512 devices in a mesh: row: 32 (over y_lo, z), col: 16 (over y_hi, x, core).
Axes of the slice: x: 4, y: 4 (y_hi: 2, y_lo: 2; y = y_hi * 2 + y_lo), z: 16, core: 2. Of those that a mesh axis runs over, the one named last changes fastest.
Arguments:
- inputs: bfloat16 [128, 1024, 2048], P('row', 'col'), may hold values from -6 to 6
- output_gradient: bfloat16 [128, 1024, 256], P('row', 'col'), may hold values from -6 to 6
- weight: bfloat16 [3, 3, 2048, 256], P(None, None, 'row'), may hold values from -0.125 to 0.125
Outputs:
- grad_in: bfloat16 [128, 1024, 2048], P('row', 'col')
- grad_weight: float32 [3, 3, 2048, 256], P(None, None, 'row')
The draws below stay inside these ranges and needn't reach their ends.
All inputs are finite; a program needn't handle non-finite values.
Results may differ from the reference program's by a relative error of at most 0.001.
Values may be sent and summed in bfloat16 or wider, within the bound.
A program may use at most 128 MiB of HBM per device.

```python
import math
import jax
import jax.numpy as jnp

CIN = 2048
COUT = 256
DILATION_STEP = 12
NH = 128
NW = 1024


def raised(entries, own_key, source, target, shards_of, factor):
    def block_of(position):
        return (jnp.arange(entries.shape[position]) // (entries.shape[position] // shards_of)).reshape((-1,) + (1,) * (entries.ndim - 1 - position))

    near = jax.random.permutation(own_key, shards_of)[block_of(target)]
    second = (block_of(target) + shards_of // 2) % shards_of
    return jnp.where((block_of(source) == near) | (block_of(source) == second), factor * entries, entries)


def steps_of(rng, dims, shards, smallest, top_value):
    factor_of = 1.0
    for axis_at, blocks in shards:
        draws = jax.random.uniform(jax.random.fold_in(jax.random.fold_in(rng, 6), axis_at), (blocks,), jnp.float32, smallest / len(shards), top_value / len(shards))
        factor_of = factor_of * jnp.repeat(jnp.exp(draws), dims[axis_at] // blocks).reshape((-1,) + (1,) * (len(dims) - 1 - axis_at))
    return factor_of


def noise(stream_key, dims, deviation, reach, cuts=(), held_as=jnp.bfloat16):
    gain = steps_of(stream_key, dims, cuts, -0.22, 0.18) if cuts else 1.0
    result = jax.random.normal(stream_key, dims, jnp.float32) * deviation * gain
    return jnp.minimum(jnp.maximum(result, -reach), reach).astype(held_as)


def gaussian_with(own_key, dims, deviation, reach, cuts, heavy, kind=jnp.bfloat16):
    drawn = deviation * jax.random.normal(own_key, dims, jnp.float32)
    if cuts:
        drawn = drawn * steps_of(own_key, dims, cuts, -0.22, 0.18)
    return jnp.clip(raised(drawn, jax.random.fold_in(own_key, 3), *heavy), -reach, reach).astype(kind)


def setup_inputs(seed: int = 0) -> dict:
    keys = jax.random.split(jax.random.key(seed), 4)
    inputs = gaussian_with(keys[0], (NH, NW, CIN), 1.0, 6.0, ((0, 32), (1, 16)), (0, 2, 32, 2.75))
    output_gradient = gaussian_with(keys[1], (NH, NW, COUT), 1.0, 6.0, ((0, 32), (1, 16)), (1, 2, 16, 2.0))
    weight = noise(keys[2], (3, 3, CIN, COUT), (9 * COUT) ** -0.5, 0.125, ((2, 32),))
    return {"inputs": inputs, "output_gradient": output_gradient, "weight": weight}


def reference(inputs, output_gradient, weight):
    height, width, in_chans = inputs.shape
    out_chans = output_gradient.shape[2]
    padded_gradient = jnp.pad(output_gradient, ((DILATION_STEP, DILATION_STEP), (DILATION_STEP, DILATION_STEP), (0, 0)))
    flat_in = inputs.reshape(height * width, in_chans)
    grad_in = jnp.zeros((height * width, in_chans), jnp.float32)
    taps = []
    for kernel_tap_row in range(3):
        for kernel_tap_column in range(3):
            top_offset = DILATION_STEP * (2 - kernel_tap_row)
            left_offset = DILATION_STEP * (2 - kernel_tap_column)
            window = padded_gradient[top_offset:top_offset + height, left_offset:left_offset + width].reshape(height * width, out_chans)
            grad_in = grad_in + jnp.dot(window, weight[kernel_tap_row, kernel_tap_column].T, preferred_element_type=jnp.float32)
            taps.append(jnp.dot(flat_in.T, window, preferred_element_type=jnp.float32))
    scale = 1.0 / math.sqrt(height * width)
    grad_weight = jnp.stack(taps).reshape(3, 3, in_chans, out_chans) * scale
    return (grad_in.reshape(height, width, in_chans).astype(jnp.bfloat16), grad_weight)
```

```python
import functools
import math

import jax
import jax.numpy as jnp
from jax import lax
from jax.experimental import pallas as pl
from jax.experimental.pallas import tpu as pltpu
from jax.sharding import PartitionSpec as P

MESH = pl.DeviceIdType.MESH
STEP = 12
PAD = 16
DZ = (-1, 0, 1, 2)


def mod(a, n):
    return lax.rem(a + 4 * n, n)


def kernel(scale, x_ref, g_ref, w_ref, gi_ref, gw_ref, gall, gs, xg, xt, wg, part, ry, ssum, rz, qsum, rl, fin, gib,
           s_g, r_g, s_f, s_h, r_h, s_x, r_x, s_w, r_w, s_y, r_y, s_z, r_z, s_l, r_l, s_a, r_a, s_o, r_o, l_sem):
    row, col = lax.axis_index("row"), lax.axis_index("col")
    z, y_lo = lax.rem(row, 16), lax.div(row, 16)
    k, y_hi = lax.rem(col, 8), lax.div(col, 8)
    x, c = lax.div(k, 2), lax.rem(k, 2)
    y = 2 * y_hi + y_lo
    sgn = 1 - 2 * c

    def dev(xx, yy, zz, cc):
        return (lax.rem(yy, 2) * 16 + zz, lax.div(yy, 2) * 8 + 2 * xx + cc)

    def ring(dx, dc):
        xx, cc = mod(x + dx, 4), mod(c + dc, 2)
        return dev(xx, y, z, cc), 2 * xx + cc

    def block(dy, dz):
        yy, zz = mod(y + dy, 4), mod(z + sgn * dz, 16)
        return dev(x, yy, zz, c), yy, zz

    own_row = 4 * k + y
    quarter, turn = lax.rem(z, 4), lax.div(z, 4)
    line_k, line_y = lax.div(row, 4), lax.rem(row, 4)
    line_q, line_s = lax.div(col, 4), lax.rem(col, 4)

    def line(m):
        return dev(lax.div(line_k, 2), line_y, 4 * m + line_q, lax.rem(line_k, 2))

    def same(d):
        return jnp.logical_and(d[0] == row, d[1] == col)

    barrier = pltpu.get_barrier_semaphore()

    def greet(d):
        pl.semaphore_signal(barrier, inc=1, device_id=d, device_id_type=MESH)

    for n in range(1, 16):
        greet((row, mod(col + n, 16)))
    for dy in range(4):
        for dz in DZ:
            if (dy, dz) != (0, 0):
                greet(block(-dy, -dz)[0])
    greet((mod(row + 3, 32), col))
    greet((mod(row - 3, 32), col))
    greet((own_row, 4 * quarter + turn))
    for m in range(4):
        greet(line(m))
    pl.semaphore_wait(barrier, 15 + 15 + 2 + 1 + 4)

    sends = []

    def send(src, dst, ss, rs, d):
        cp = pltpu.make_async_remote_copy(src_ref=src, dst_ref=dst, send_sem=ss, recv_sem=rs, device_id=d, device_id_type=MESH)
        cp.start()
        sends.append(cp)

    def arrived(dst, rs):
        pltpu.make_async_remote_copy(src_ref=dst, dst_ref=dst, send_sem=rs, recv_sem=rs, device_id=ring(0, 1)[0], device_id_type=MESH).wait_recv()

    def gpiece(t, kk):
        return gall.at[t, :, pl.ds(pl.multiple_of(PAD + 64 * kk, 16), 64), :]

    def xpiece(ref, kk):
        return ref.at[:, pl.ds(pl.multiple_of(64 * kk, 64), 64), :]

    def chans(ref, kk):
        return ref.at[:, :, pl.ds(pl.multiple_of(256 * kk, 256), 256)]

    def wpiece(i, p):
        return wg.at[:, pl.ds(pl.multiple_of(64 * i + 16 * p, 16), 16), :]

    send(g_ref, gpiece(0, k), s_g.at[0, 0], r_g.at[0, 0, 0], (mod(row + 3, 32), col))
    send(g_ref, gpiece(2, k), s_g.at[2, 0], r_g.at[2, 0, 0], (mod(row - 3, 32), col))
    own_g = pltpu.make_async_copy(g_ref, gpiece(1, k), r_g.at[1, 0, 0])
    own_g.start()
    w_to = (line(line_s), line_y, line_q)
    w_src = w_ref.at[:, pl.ds(pl.multiple_of(16 * line_q, 16), 16), :]
    w_self = same(w_to[0])
    w_remote = pltpu.make_async_remote_copy(src_ref=w_src, dst_ref=wpiece(line_y, line_q), send_sem=s_w.at[0, 1], recv_sem=r_w.at[0, 1], device_id=w_to[0], device_id_type=MESH)

    @pl.when(jnp.logical_not(w_self))
    def _():
        w_remote.start()

    @pl.when(w_self)
    def _():
        pltpu.make_async_copy(w_src, wpiece(line_y, line_q), r_w.at[0, 1]).start()

    is_edge = jnp.logical_or(jnp.logical_and(y_hi == 1, k == 0), jnp.logical_and(y_hi == 0, k == 7))
    edge_from = jnp.where(y_hi == 1, 0, 48)
    edge_to = jnp.where(y_hi == 1, PAD + 512, 0)
    other = 1 - y_hi

    def strip_copy(t, kk):
        src = gall.at[t, :, pl.ds(pl.multiple_of(PAD + 64 * k + edge_from, 16), 16), :]
        dst = gall.at[t, :, pl.ds(pl.multiple_of(edge_to, 16), 16), :]
        return pltpu.make_async_remote_copy(src_ref=src, dst_ref=dst, send_sem=s_h.at[t, kk], recv_sem=r_h.at[t], device_id=(row, 8 * other + kk), device_id_type=MESH)

    def spread(t):
        src = gpiece(t, k)
        for dx in (1, 3, 2):
            send(src, gpiece(t, k), s_f.at[t, dx], r_g.at[t, dx, 0], ring(dx, 0)[0])
        send(src, gpiece(t, k), s_f.at[t, 0], r_g.at[t, 0, 1], ring(0, 1)[0])

        @pl.when(is_edge)
        def _():
            for kk in range(8):
                strip_copy(t, kk).start()

    def hand_over(t):
        for dx in (1, 3, 2):
            kk = ring(-dx, 0)[1]
            arrived(gpiece(t, kk), r_g.at[t, dx, 0])
            send(gpiece(t, kk), gpiece(t, kk), s_g.at[t, dx], r_g.at[t, dx, 1], ring(0, 1)[0])

    own_g.wait()
    spread(1)
    for dx, dc in ((1, 0), (3, 0), (1, 1), (3, 1), (2, 0), (2, 1), (0, 1)):
        to, kk = ring(dx, dc)
        send(chans(x_ref, kk), xpiece(xg, k), s_x.at[dx, dc], r_x.at[dx, dc], to)
    own_x = pltpu.make_async_copy(chans(x_ref, k), xpiece(xg, k), r_x.at[0, 0])
    own_x.start()

    @pl.when(y_hi == 0)
    def _():
        gall[:, :, 0:PAD, :] = jnp.zeros((3, 4, PAD, 256), gall.dtype)

    @pl.when(y_hi == 1)
    def _():
        gall[:, :, PAD + 512 :, :] = jnp.zeros((3, 4, PAD, 256), gall.dtype)

    arrived(wpiece(y, quarter), r_w.at[0, 1])
    for dy in (1, 3, 2, 0):
        for dz in DZ:
            if (dy, dz) != (0, 0):
                send(wpiece(y, quarter), wpiece(y, quarter), s_w.at[dy, dz + 1], r_w2(r_w, dy, dz), block(dy, dz)[0])
    for t in (0, 2):
        arrived(gpiece(t, k), r_g.at[t, 0, 0])
        spread(t)
    hand_over(1)

    def tile_ready(t):
        for dx in range(4):
            arrived(gpiece(t, ring(-dx, 1)[1]), r_g.at[t, dx, 1])
        arrived(gall.at[t, :, pl.ds(pl.multiple_of(jnp.where(y_hi == 1, 0, PAD + 512), 16), 16), :], r_h.at[t])

    def shifts(t):
        valid = {0: row >= 3, 1: row >= 0, 2: row < 29}[t]

        def body(h, carry):
            for b in range(3):
                off = PAD + STEP * (1 - b)
                v = gall[t, h, off : off + 512, :]
                gs[t, b, pl.ds(pl.multiple_of(512 * h, 512), 512), :] = jnp.where(valid, v, jnp.zeros_like(v))
            return carry

        lax.fori_loop(0, 4, body, 0)

    def filter_terms(t):
        a = 2 - t

        def body(b, carry):
            part[a, b] = jnp.dot(xt[...], gs[t, b], preferred_element_type=jnp.float32)
            return carry

        lax.fori_loop(0, 3, body, 0)
        for dy in (1, 3, 2):
            to, yy, _ = block(dy, 0)
            send(part.at[a, :, pl.ds(pl.multiple_of(64 * yy, 64), 64), :], ry.at[a, dy - 1], s_y.at[a, dy], r_y.at[a, dy], to)

    own_x.wait()
    for dx, dc in ((1, 0), (3, 0), (1, 1), (3, 1), (2, 0), (2, 1), (0, 1)):
        arrived(xpiece(xg, ring(-dx, -dc)[1]), r_x.at[dx, dc])

    for h in range(4):
        xt[:, 512 * h : 512 * h + 512] = xg[h].T
    tile_ready(1)
    shifts(1)
    filter_terms(1)
    for t in (0, 2):
        hand_over(t)
    for t in (0, 2):
        tile_ready(t)
        shifts(t)
        filter_terms(t)

    for dy in (1, 3, 2, 0):
        for dz in DZ:
            if (dy, dz) != (0, 0):
                _, yy, zz = block(-dy, -dz)
                arrived(wpiece(yy, lax.rem(zz, 4)), r_w2(r_w, dy, dz))

    def back(h, carry):
        rows = pl.ds(pl.multiple_of(512 * h, 512), 512)
        total = jnp.zeros((512, 256), jnp.float32)
        for t in range(3):
            for b in range(3):
                total = total + lax.dot_general(
                    gs[t, b, rows, :], wg[3 * (2 - t) + b], (((1,), (1,)), ((), ())), preferred_element_type=jnp.float32
                )
        gib[h] = total.astype(gib.dtype)
        return carry

    lax.fori_loop(0, 4, back, 0)
    for dx, dc in ((1, 0), (3, 0), (1, 1), (3, 1), (2, 0), (2, 1), (0, 1)):
        to, kk = ring(dx, dc)
        send(xpiece(gib, kk), chans(gi_ref, k), s_o.at[dx, dc], r_o.at[dx, dc], to)
    own_o = pltpu.make_async_copy(xpiece(gib, k), chans(gi_ref, k), r_o.at[0, 0])
    own_o.start()

    for a in (1, 2, 0):
        for dy in (1, 3, 2):
            arrived(ry.at[a, dy - 1], r_y.at[a, dy])
        mine = part[a, :, pl.ds(pl.multiple_of(64 * y, 64), 64), :]
        ssum[a] = mine + ry[a, 0] + ry[a, 1] + ry[a, 2]
        for n, dz in enumerate((-1, 1, 2)):
            to, _, zz = block(0, dz)
            q = lax.rem(zz, 4)
            send(ssum.at[a, :, pl.ds(pl.multiple_of(16 * q, 16), 16), :], rz.at[a, n], s_z.at[a, n], r_z.at[a, n], to)
    for a in (1, 2, 0):
        for n in range(3):
            arrived(rz.at[a, n], r_z.at[a, n])
        mine = ssum[a, :, pl.ds(pl.multiple_of(16 * quarter, 16), 16), :]
        qsum[3 * a : 3 * a + 3] = mine + rz[a, 0] + rz[a, 1] + rz[a, 2]

    owners = []
    for s in range(4):
        to = (own_row, 4 * quarter + s)
        src = qsum.at[:, 8 * (s // 2) : 8 * (s // 2) + 8, 128 * (s % 2) : 128 * (s % 2) + 128]
        cp = pltpu.make_async_remote_copy(src_ref=src, dst_ref=rl.at[turn], send_sem=s_l.at[s], recv_sem=r_l.at[turn], device_id=to, device_id_type=MESH)
        me = same(to)

        @pl.when(jnp.logical_not(me))
        def _():
            cp.start()

        @pl.when(me)
        def _():
            pltpu.make_async_copy(src, rl.at[turn], r_l.at[turn]).start()

        owners.append((cp, me))
    for m in range(4):
        arrived(rl.at[m], r_l.at[m])
    fin[...] = (rl[0] + rl[1] + rl[2] + rl[3]) * scale

    def slot(cc):
        return gw_ref.at[
            :,
            pl.ds(pl.multiple_of(16 * lax.div(cc, 4) + 8 * lax.div(lax.rem(cc, 4), 2), 8), 8),
            pl.ds(pl.multiple_of(128 * lax.rem(cc, 2), 128), 128),
        ]

    for n in range(1, 16):
        send(fin, slot(col), s_a.at[n], r_a.at[n], (row, mod(col + n, 16)))
    own_f = pltpu.make_async_copy(fin, slot(col), l_sem)
    own_f.start()

    for dx, dc in ((1, 0), (3, 0), (1, 1), (3, 1), (2, 0), (2, 1), (0, 1)):
        arrived(chans(gi_ref, ring(-dx, -dc)[1]), r_o.at[dx, dc])
    own_o.wait()
    for n in range(1, 16):
        arrived(slot(mod(col - n, 16)), r_a.at[n])
    own_f.wait()
    for cp in sends:
        cp.wait_send()

    @pl.when(jnp.logical_not(w_self))
    def _():
        w_remote.wait_send()

    for cp, me in owners:

        @pl.when(jnp.logical_not(me))
        def _():
            cp.wait_send()

    @pl.when(is_edge)
    def _():
        for t in range(3):
            for kk in range(8):
                strip_copy(t, kk).wait_send()


def r_w2(r_w, dy, dz):
    return r_w.at[dy, dz + 1]


def shards(inputs, output_gradient, weight):
    height, width, in_chans = inputs.shape
    total = height * width * lax.axis_size("row") * lax.axis_size("col")
    bf, f32 = jnp.bfloat16, jnp.float32
    dma = pltpu.SemaphoreType.DMA
    scratch = [
        pltpu.VMEM((3, 4, 2 * PAD + 512, 256), bf),
        pltpu.VMEM((3, 3, 2048, 256), bf),
        pltpu.VMEM((4, 512, 256), bf),
        pltpu.VMEM((256, 2048), bf),
        pltpu.VMEM((9, 256, 256), bf),
        pltpu.VMEM((3, 3, 256, 256), f32),
        pltpu.VMEM((3, 3, 3, 64, 256), f32),
        pltpu.VMEM((3, 3, 64, 256), f32),
        pltpu.VMEM((3, 3, 3, 16, 256), f32),
        pltpu.VMEM((9, 16, 256), f32),
        pltpu.VMEM((4, 9, 8, 128), f32),
        pltpu.VMEM((9, 8, 128), f32),
        pltpu.VMEM((4, 512, 256), bf),
        dma((3, 4)), dma((3, 4, 2)), dma((3, 4)), dma((3, 8)), dma((3,)),
        dma((4, 2)), dma((4, 2)), dma((4, 4)), dma((4, 4)),
        dma((3, 4)), dma((3, 4)), dma((3, 3)), dma((3, 3)),
        dma((4,)), dma((4,)), dma((16,)), dma((16,)), dma((4, 2)), dma((4, 2)), dma,
    ]
    hbm = pl.BlockSpec(memory_space=pl.ANY)
    grad_in, grad_weight = pl.pallas_call(
        functools.partial(kernel, 1.0 / math.sqrt(total)),
        out_shape=(jax.ShapeDtypeStruct(inputs.shape, bf), jax.ShapeDtypeStruct((9,) + weight.shape[2:], f32)),
        in_specs=[hbm] * 3,
        out_specs=(hbm, hbm),
        scratch_shapes=scratch,
        compiler_params=pltpu.CompilerParams(collective_id=0, has_side_effects=True, vmem_limit_bytes=56 * 1024 * 1024),
    )(inputs, output_gradient, weight.reshape((9,) + weight.shape[2:]))
    return grad_in, grad_weight.reshape(weight.shape)


def solution(mesh):
    return jax.shard_map(
        shards,
        mesh=mesh,
        in_specs=(P("row", "col", None), P("row", "col", None), P(None, None, "row", None)),
        out_specs=(P("row", "col", None), P(None, None, "row", None)),
        check_vma=False,
    )
```

```python
import functools
import math

import jax
import jax.numpy as jnp
from jax import lax
from jax.experimental import pallas as pl
from jax.experimental.pallas import tpu as pltpu
from jax.sharding import PartitionSpec as P

MESH = pl.DeviceIdType.MESH
STEP = 12
PAD = 16
DZ = (-1, 0, 1, 2)


def mod(a, n):
    return lax.rem(a + 4 * n, n)


def kernel(scale, x_ref, g_ref, w_ref, gi_ref, gw_ref, gall, gs, xg, xt, wg, part, ry, rz, suma, sumb, rz2, ry2, qsum, rl, rm, fin, gib,
           s_g, r_g, s_f, s_h, r_h, s_x, r_x, s_w, r_w, s_y, r_y, s_z, r_z, s_y2, r_y2, s_z2, r_z2, s_l, r_l, s_m, r_m, s_a, r_a, s_o, r_o, l_sem):
    row, col = lax.axis_index("row"), lax.axis_index("col")
    z, y_lo = lax.rem(row, 16), lax.div(row, 16)
    k, y_hi = lax.rem(col, 8), lax.div(col, 8)
    x, c = lax.div(k, 2), lax.rem(k, 2)
    y = 2 * y_hi + y_lo
    sgn = 1 - 2 * c

    def dev(xx, yy, zz, cc):
        return (lax.rem(yy, 2) * 16 + zz, lax.div(yy, 2) * 8 + 2 * xx + cc)

    def ring(dx, dc):
        xx, cc = mod(x + dx, 4), mod(c + dc, 2)
        return dev(xx, y, z, cc), 2 * xx + cc

    def block(dy, dz):
        yy, zz = mod(y + dy, 4), mod(z + sgn * dz, 16)
        return dev(x, yy, zz, c), yy, zz

    quarter, turn = lax.rem(z, 4), lax.div(z, 4)
    line_k, line_y = lax.div(row, 4), lax.rem(row, 4)
    line_q, line_s = lax.div(col, 4), lax.rem(col, 4)

    def line(m):
        return dev(lax.div(line_k, 2), line_y, 4 * m + line_q, lax.rem(line_k, 2))

    def holder(m):
        kk = 4 * y_lo + m
        return dev(lax.div(kk, 2), lax.div(col, 4), z, lax.rem(kk, 2))

    def along(n):
        return dev(x, y, mod(z + 4 * n, 16), c)

    def same(d):
        return jnp.logical_and(d[0] == row, d[1] == col)

    barrier = pltpu.get_barrier_semaphore()

    def greet(d):
        pl.semaphore_signal(barrier, inc=1, device_id=d, device_id_type=MESH)

    for n in range(1, 16):
        greet((row, mod(col + n, 16)))
    for dy in range(4):
        for dz in DZ:
            if (dy, dz) != (0, 0):
                greet(block(-dy, -dz)[0])
    greet((mod(row + 3, 32), col))
    greet((mod(row - 3, 32), col))
    greet((4 * k + y, 4 * quarter + turn))
    for m in range(4):
        greet(holder(m))
    for n in range(1, 4):
        greet(along(-n))
    pl.semaphore_wait(barrier, 15 + 15 + 2 + 1 + 4 + 3)

    sends = []

    def send(src, dst, ss, rs, d):
        cp = pltpu.make_async_remote_copy(src_ref=src, dst_ref=dst, send_sem=ss, recv_sem=rs, device_id=d, device_id_type=MESH)
        cp.start()
        sends.append(cp)

    def arrived(dst, rs):
        pltpu.make_async_remote_copy(src_ref=dst, dst_ref=dst, send_sem=rs, recv_sem=rs, device_id=ring(0, 1)[0], device_id_type=MESH).wait_recv()

    def gpiece(t, kk):
        return gall.at[t, :, pl.ds(pl.multiple_of(PAD + 64 * kk, 16), 64), :]

    def xpiece(ref, kk):
        return ref.at[:, pl.ds(pl.multiple_of(64 * kk, 64), 64), :]

    def chans(ref, kk):
        return ref.at[:, :, pl.ds(pl.multiple_of(256 * kk, 256), 256)]

    def wpiece(i, p):
        return wg.at[:, pl.ds(pl.multiple_of(64 * i + 16 * p, 16), 16), :]

    send(g_ref, gpiece(0, k), s_g.at[0, 0], r_g.at[0, 0, 0], (mod(row + 3, 32), col))
    send(g_ref, gpiece(2, k), s_g.at[2, 0], r_g.at[2, 0, 0], (mod(row - 3, 32), col))
    own_g = pltpu.make_async_copy(g_ref, gpiece(1, k), r_g.at[1, 0, 0])
    own_g.start()
    w_to = (line(line_s), line_y, line_q)
    w_src = w_ref.at[:, pl.ds(pl.multiple_of(16 * line_q, 16), 16), :]
    w_self = same(w_to[0])
    w_remote = pltpu.make_async_remote_copy(src_ref=w_src, dst_ref=wpiece(line_y, line_q), send_sem=s_w.at[0, 1], recv_sem=r_w.at[0, 1], device_id=w_to[0], device_id_type=MESH)

    @pl.when(jnp.logical_not(w_self))
    def _():
        w_remote.start()

    @pl.when(w_self)
    def _():
        pltpu.make_async_copy(w_src, wpiece(line_y, line_q), r_w.at[0, 1]).start()

    is_edge = jnp.logical_or(jnp.logical_and(y_hi == 1, k == 0), jnp.logical_and(y_hi == 0, k == 7))
    edge_from = jnp.where(y_hi == 1, 0, 48)
    edge_to = jnp.where(y_hi == 1, PAD + 512, 0)
    other = 1 - y_hi

    def strip_copy(t, kk):
        if t == 1:
            src = g_ref.at[:, pl.ds(pl.multiple_of(edge_from, 16), 16), :]
        else:
            src = gall.at[t, :, pl.ds(pl.multiple_of(PAD + 64 * k + edge_from, 16), 16), :]
        dst = gall.at[t, :, pl.ds(pl.multiple_of(edge_to, 16), 16), :]
        return pltpu.make_async_remote_copy(src_ref=src, dst_ref=dst, send_sem=s_h.at[t, kk], recv_sem=r_h.at[t], device_id=(row, 8 * other + kk), device_id_type=MESH)

    def spread(t):
        src = g_ref if t == 1 else gpiece(t, k)
        for dx in (1, 3, 2):
            send(src, gpiece(t, k), s_f.at[t, dx], r_g.at[t, dx, 0], ring(dx, 0)[0])
        send(src, gpiece(t, k), s_f.at[t, 0], r_g.at[t, 0, 1], ring(0, 1)[0])

        @pl.when(is_edge)
        def _():
            for kk in range(8):
                strip_copy(t, kk).start()

    def hand_over(t):
        for dx in (1, 3, 2):
            kk = ring(-dx, 0)[1]
            arrived(gpiece(t, kk), r_g.at[t, dx, 0])
            send(gpiece(t, kk), gpiece(t, kk), s_g.at[t, dx], r_g.at[t, dx, 1], ring(0, 1)[0])

    spread(1)
    for dx, dc in ((1, 0), (3, 0), (1, 1), (3, 1), (2, 0), (2, 1), (0, 1)):
        to, kk = ring(dx, dc)
        send(chans(x_ref, kk), xpiece(xg, k), s_x.at[dx, dc], r_x.at[dx, dc], to)
    own_x = pltpu.make_async_copy(chans(x_ref, k), xpiece(xg, k), r_x.at[0, 0])
    own_x.start()

    @pl.when(y_hi == 0)
    def _():
        gall[:, :, 0:PAD, :] = jnp.zeros((3, 4, PAD, 256), gall.dtype)

    @pl.when(y_hi == 1)
    def _():
        gall[:, :, PAD + 512 :, :] = jnp.zeros((3, 4, PAD, 256), gall.dtype)

    arrived(wpiece(y, quarter), r_w.at[0, 1])
    for dy in (1, 3, 2, 0):
        for dz in DZ:
            if (dy, dz) != (0, 0):
                send(wpiece(y, quarter), wpiece(y, quarter), s_w.at[dy, dz + 1], r_w2(r_w, dy, dz), block(dy, dz)[0])
    hand_over(1)
    for t in (0, 2):
        arrived(gpiece(t, k), r_g.at[t, 0, 0])
        spread(t)
    own_g.wait()

    def tile_ready(t):
        for dx in range(4):
            arrived(gpiece(t, ring(-dx, 1)[1]), r_g.at[t, dx, 1])
        arrived(gall.at[t, :, pl.ds(pl.multiple_of(jnp.where(y_hi == 1, 0, PAD + 512), 16), 16), :], r_h.at[t])

    def shifts(t):
        valid = {0: row >= 3, 1: row >= 0, 2: row < 29}[t]

        def body(h, carry):
            for b in range(3):
                off = PAD + STEP * (1 - b)
                v = gall[t, h, off : off + 512, :]
                gs[t, b, pl.ds(pl.multiple_of(512 * h, 512), 512), :] = jnp.where(valid, v, jnp.zeros_like(v))
            return carry

        lax.fori_loop(0, 4, body, 0)

    def filter_terms(t):
        a = 2 - t

        def body(b, carry):
            part[a, b] = jnp.dot(xt[...], gs[t, b], preferred_element_type=jnp.float32).reshape(4, 4, 16, 256)
            return carry

        lax.fori_loop(0, 3, body, 0)
        for dy in (1, 3, 2):
            to, yy, _ = block(dy, 0)
            send(part.at[a, :, :, yy, :, 0:128], ry.at[a, dy - 1], s_y.at[a, dy], r_y.at[a, dy], to)
        for n, dz in enumerate((-1, 1, 2)):
            to, _, zz = block(0, dz)
            send(part.at[a, :, lax.rem(zz, 4), :, :, 128:256], rz.at[a, n], s_z.at[a, n], r_z.at[a, n], to)

    def first_sums(a):
        for dy in (1, 3, 2):
            arrived(ry.at[a, dy - 1], r_y.at[a, dy])
        suma[a] = part[a, :, :, y, :, 0:128] + ry[a, 0] + ry[a, 1] + ry[a, 2]
        for n, dz in enumerate((-1, 1, 2)):
            to, _, zz = block(0, dz)
            send(suma.at[a, :, lax.rem(zz, 4)], rz2.at[a, n], s_z2.at[a, n], r_z2.at[a, n], to)
        for n in range(3):
            arrived(rz.at[a, n], r_z.at[a, n])
        sumb[a] = part[a, :, quarter, :, :, 128:256] + rz[a, 0] + rz[a, 1] + rz[a, 2]
        for dy in (1, 3, 2):
            to, yy, _ = block(dy, 0)
            send(sumb.at[a, :, yy], ry2.at[a, dy - 1], s_y2.at[a, dy], r_y2.at[a, dy], to)

    def second_sums(a):
        for n in range(3):
            arrived(rz2.at[a, n], r_z2.at[a, n])
        qsum[3 * a : 3 * a + 3, :, 0:128] = suma[a, :, quarter] + rz2[a, 0] + rz2[a, 1] + rz2[a, 2]
        for dy in (1, 3, 2):
            arrived(ry2.at[a, dy - 1], r_y2.at[a, dy])
        qsum[3 * a : 3 * a + 3, :, 128:256] = sumb[a, :, y] + ry2[a, 0] + ry2[a, 1] + ry2[a, 2]

    own_x.wait()
    for dx, dc in ((1, 0), (3, 0), (1, 1), (3, 1), (2, 0), (2, 1), (0, 1)):
        arrived(xpiece(xg, ring(-dx, -dc)[1]), r_x.at[dx, dc])

    for h in range(4):
        xt[:, 512 * h : 512 * h + 512] = xg[h].T
    tile_ready(1)
    shifts(1)
    filter_terms(1)
    for t in (0, 2):
        hand_over(t)
    tile_ready(0)
    shifts(0)
    filter_terms(0)
    first_sums(1)
    tile_ready(2)
    shifts(2)
    filter_terms(2)

    for dy in (1, 3, 2, 0):
        for dz in DZ:
            if (dy, dz) != (0, 0):
                _, yy, zz = block(-dy, -dz)
                arrived(wpiece(yy, lax.rem(zz, 4)), r_w2(r_w, dy, dz))

    def back(h, carry):
        rows = pl.ds(pl.multiple_of(512 * h, 512), 512)
        total = jnp.zeros((512, 256), jnp.float32)
        for t in range(3):
            for b in range(3):
                total = total + lax.dot_general(
                    gs[t, b, rows, :], wg[3 * (2 - t) + b], (((1,), (1,)), ((), ())), preferred_element_type=jnp.float32
                )
        gib[h] = total.astype(gib.dtype)
        return carry

    lax.fori_loop(0, 4, back, 0)
    for dx, dc in ((1, 0), (3, 0), (1, 1), (3, 1), (2, 0), (2, 1), (0, 1)):
        to, kk = ring(dx, dc)
        send(xpiece(gib, kk), chans(gi_ref, k), s_o.at[dx, dc], r_o.at[dx, dc], to)
    own_o = pltpu.make_async_copy(xpiece(gib, k), chans(gi_ref, k), r_o.at[0, 0])
    own_o.start()

    first_sums(2)
    second_sums(1)
    first_sums(0)
    second_sums(2)
    second_sums(0)

    passed = []
    for s in range(4):
        to = (16 * lax.div(k, 4) + z, 4 * y + s)
        slot_k = lax.rem(k, 4)
        src = qsum.at[:, 8 * (s // 2) : 8 * (s // 2) + 8, 128 * (s % 2) : 128 * (s % 2) + 128]
        cp = pltpu.make_async_remote_copy(src_ref=src, dst_ref=rl.at[slot_k], send_sem=s_l.at[s], recv_sem=r_l.at[slot_k], device_id=to, device_id_type=MESH)
        me = same(to)

        @pl.when(jnp.logical_not(me))
        def _():
            cp.start()

        @pl.when(me)
        def _():
            pltpu.make_async_copy(src, rl.at[slot_k], r_l.at[slot_k]).start()

        passed.append((cp, me))
    for m in range(4):
        arrived(rl.at[m], r_l.at[m])
    for n in range(1, 4):
        send(rl.at[lax.rem(turn + n, 4)], rm.at[n - 1], s_m.at[n], r_m.at[n], along(n))
    for n in range(1, 4):
        arrived(rm.at[n - 1], r_m.at[n])
    fin[...] = (rl[turn] + rm[0] + rm[1] + rm[2]) * scale

    def slot(cc):
        return gw_ref.at[
            :,
            pl.ds(pl.multiple_of(16 * lax.div(cc, 4) + 8 * lax.div(lax.rem(cc, 4), 2), 8), 8),
            pl.ds(pl.multiple_of(128 * lax.rem(cc, 2), 128), 128),
        ]

    for n in range(1, 16):
        send(fin, slot(col), s_a.at[n], r_a.at[n], (row, mod(col + n, 16)))
    own_f = pltpu.make_async_copy(fin, slot(col), l_sem)
    own_f.start()

    for dx, dc in ((1, 0), (3, 0), (1, 1), (3, 1), (2, 0), (2, 1), (0, 1)):
        arrived(chans(gi_ref, ring(-dx, -dc)[1]), r_o.at[dx, dc])
    own_o.wait()
    for n in range(1, 16):
        arrived(slot(mod(col - n, 16)), r_a.at[n])
    own_f.wait()
    for cp in sends:
        cp.wait_send()

    @pl.when(jnp.logical_not(w_self))
    def _():
        w_remote.wait_send()

    for cp, me in passed:

        @pl.when(jnp.logical_not(me))
        def _():
            cp.wait_send()

    @pl.when(is_edge)
    def _():
        for t in range(3):
            for kk in range(8):
                strip_copy(t, kk).wait_send()


def r_w2(r_w, dy, dz):
    return r_w.at[dy, dz + 1]


def shards(inputs, output_gradient, weight):
    height, width, in_chans = inputs.shape
    total = height * width * lax.axis_size("row") * lax.axis_size("col")
    bf, f32 = jnp.bfloat16, jnp.float32
    dma = pltpu.SemaphoreType.DMA
    scratch = [
        pltpu.VMEM((3, 4, 2 * PAD + 512, 256), bf),
        pltpu.VMEM((3, 3, 2048, 256), bf),
        pltpu.VMEM((4, 512, 256), bf),
        pltpu.VMEM((256, 2048), bf),
        pltpu.VMEM((9, 256, 256), bf),
        pltpu.VMEM((3, 3, 4, 4, 16, 256), f32),
        pltpu.VMEM((3, 3, 3, 4, 16, 128), f32),
        pltpu.VMEM((3, 3, 3, 4, 16, 128), f32),
        pltpu.VMEM((3, 3, 4, 16, 128), f32),
        pltpu.VMEM((3, 3, 4, 16, 128), f32),
        pltpu.VMEM((3, 3, 3, 16, 128), f32),
        pltpu.VMEM((3, 3, 3, 16, 128), f32),
        pltpu.VMEM((9, 16, 256), f32),
        pltpu.VMEM((4, 9, 8, 128), f32),
        pltpu.VMEM((3, 9, 8, 128), f32),
        pltpu.VMEM((9, 8, 128), f32),
        pltpu.VMEM((4, 512, 256), bf),
        dma((3, 4)), dma((3, 4, 2)), dma((3, 4)), dma((3, 8)), dma((3,)),
        dma((4, 2)), dma((4, 2)), dma((4, 4)), dma((4, 4)),
        dma((3, 4)), dma((3, 4)), dma((3, 3)), dma((3, 3)), dma((3, 4)), dma((3, 4)), dma((3, 3)), dma((3, 3)),
        dma((4,)), dma((4,)), dma((4,)), dma((4,)), dma((16,)), dma((16,)), dma((4, 2)), dma((4, 2)), dma,
    ]
    hbm = pl.BlockSpec(memory_space=pl.ANY)
    grad_in, grad_weight = pl.pallas_call(
        functools.partial(kernel, 1.0 / math.sqrt(total)),
        out_shape=(jax.ShapeDtypeStruct(inputs.shape, bf), jax.ShapeDtypeStruct((9,) + weight.shape[2:], f32)),
        in_specs=[hbm] * 3,
        out_specs=(hbm, hbm),
        scratch_shapes=scratch,
        compiler_params=pltpu.CompilerParams(collective_id=0, has_side_effects=True, vmem_limit_bytes=56 * 1024 * 1024),
    )(inputs, output_gradient, weight.reshape((9,) + weight.shape[2:]))
    return grad_in, grad_weight.reshape(weight.shape)


def solution(mesh):
    return jax.shard_map(
        shards,
        mesh=mesh,
        in_specs=(P("row", "col", None), P("row", "col", None), P(None, None, "row", None)),
        out_specs=(P("row", "col", None), P(None, None, "row", None)),
        check_vma=False,
    )
```

```python
import functools
import math

import jax
import jax.numpy as jnp
from jax import lax
from jax.experimental import pallas as pl
from jax.experimental.pallas import tpu as pltpu
from jax.sharding import PartitionSpec as P

MESH = pl.DeviceIdType.MESH
STEP = 12
PAD = 16
DZ = (-1, 0, 1, 2)


def mod(a, n):
    return lax.rem(a + 4 * n, n)


def kernel(scale, x_ref, g_ref, w_ref, gi_ref, gw_ref, gall, gs, xg, xt, wg, part, ry, rz, suma, sumb, rz2, ry2, qsum, rl, fin, gib,
           s_g, r_g, s_f, s_h, r_h, s_x, r_x, s_w, r_w, s_y, r_y, s_z, r_z, s_y2, r_y2, s_z2, r_z2, s_l, r_l, s_a, r_a, s_o, r_o, l_sem):
    row, col = lax.axis_index("row"), lax.axis_index("col")
    z, y_lo = lax.rem(row, 16), lax.div(row, 16)
    k, y_hi = lax.rem(col, 8), lax.div(col, 8)
    x, c = lax.div(k, 2), lax.rem(k, 2)
    y = 2 * y_hi + y_lo
    sgn = 1 - 2 * c

    def dev(xx, yy, zz, cc):
        return (lax.rem(yy, 2) * 16 + zz, lax.div(yy, 2) * 8 + 2 * xx + cc)

    def ring(dx, dc):
        xx, cc = mod(x + dx, 4), mod(c + dc, 2)
        return dev(xx, y, z, cc), 2 * xx + cc

    def block(dy, dz):
        yy, zz = mod(y + dy, 4), mod(z + sgn * dz, 16)
        return dev(x, yy, zz, c), yy, zz

    quarter, turn = lax.rem(z, 4), lax.div(z, 4)
    line_k, line_y = lax.div(row, 4), lax.rem(row, 4)
    line_q, line_s = lax.div(col, 4), lax.rem(col, 4)

    def line(m):
        return dev(lax.div(line_k, 2), line_y, 4 * m + line_q, lax.rem(line_k, 2))

    def holder(m):
        kk = lax.div(row, 4)
        return dev(lax.div(kk, 2), lax.div(col, 4), 4 * m + quarter, lax.rem(kk, 2))

    def same(d):
        return jnp.logical_and(d[0] == row, d[1] == col)

    barrier = pltpu.get_barrier_semaphore()

    def greet(d):
        pl.semaphore_signal(barrier, inc=1, device_id=d, device_id_type=MESH)

    for n in range(1, 16):
        greet((row, mod(col + n, 16)))
    for dy in range(4):
        for dz in DZ:
            if (dy, dz) != (0, 0):
                greet(block(-dy, -dz)[0])
    greet((mod(row + 3, 32), col))
    greet((mod(row - 3, 32), col))
    greet((4 * k + y, 4 * quarter + turn))
    for m in range(4):
        greet(holder(m))
    pl.semaphore_wait(barrier, 15 + 15 + 2 + 1 + 4)

    sends = []

    def send(src, dst, ss, rs, d):
        cp = pltpu.make_async_remote_copy(src_ref=src, dst_ref=dst, send_sem=ss, recv_sem=rs, device_id=d, device_id_type=MESH)
        cp.start()
        sends.append(cp)

    def arrived(dst, rs):
        pltpu.make_async_remote_copy(src_ref=dst, dst_ref=dst, send_sem=rs, recv_sem=rs, device_id=ring(0, 1)[0], device_id_type=MESH).wait_recv()

    def gpiece(t, kk):
        return gall.at[t, :, pl.ds(pl.multiple_of(PAD + 64 * kk, 16), 64), :]

    def xpiece(ref, kk):
        return ref.at[:, pl.ds(pl.multiple_of(64 * kk, 64), 64), :]

    def chans(ref, kk):
        return ref.at[:, :, pl.ds(pl.multiple_of(256 * kk, 256), 256)]

    def wpiece(i, p):
        return wg.at[:, pl.ds(pl.multiple_of(64 * i + 16 * p, 16), 16), :]

    send(g_ref, gpiece(0, k), s_g.at[0, 0], r_g.at[0, 0, 0], (mod(row + 3, 32), col))
    send(g_ref, gpiece(2, k), s_g.at[2, 0], r_g.at[2, 0, 0], (mod(row - 3, 32), col))
    own_g = pltpu.make_async_copy(g_ref, gpiece(1, k), r_g.at[1, 0, 0])
    own_g.start()
    w_to = (line(line_s), line_y, line_q)
    w_src = w_ref.at[:, pl.ds(pl.multiple_of(16 * line_q, 16), 16), :]
    w_self = same(w_to[0])
    w_remote = pltpu.make_async_remote_copy(src_ref=w_src, dst_ref=wpiece(line_y, line_q), send_sem=s_w.at[0, 1], recv_sem=r_w.at[0, 1], device_id=w_to[0], device_id_type=MESH)

    @pl.when(jnp.logical_not(w_self))
    def _():
        w_remote.start()

    @pl.when(w_self)
    def _():
        pltpu.make_async_copy(w_src, wpiece(line_y, line_q), r_w.at[0, 1]).start()

    is_edge = jnp.logical_or(jnp.logical_and(y_hi == 1, k == 0), jnp.logical_and(y_hi == 0, k == 7))
    edge_from = jnp.where(y_hi == 1, 0, 48)
    edge_to = jnp.where(y_hi == 1, PAD + 512, 0)
    other = 1 - y_hi

    def strip_copy(t, kk):
        if t == 1:
            src = g_ref.at[:, pl.ds(pl.multiple_of(edge_from, 16), 16), :]
        else:
            src = gall.at[t, :, pl.ds(pl.multiple_of(PAD + 64 * k + edge_from, 16), 16), :]
        dst = gall.at[t, :, pl.ds(pl.multiple_of(edge_to, 16), 16), :]
        return pltpu.make_async_remote_copy(src_ref=src, dst_ref=dst, send_sem=s_h.at[t, kk], recv_sem=r_h.at[t], device_id=(row, 8 * other + kk), device_id_type=MESH)

    def spread(t):
        src = g_ref if t == 1 else gpiece(t, k)
        for dx in (1, 3, 2):
            send(src, gpiece(t, k), s_f.at[t, dx], r_g.at[t, dx, 0], ring(dx, 0)[0])
        send(src, gpiece(t, k), s_f.at[t, 0], r_g.at[t, 0, 1], ring(0, 1)[0])

        @pl.when(is_edge)
        def _():
            for kk in range(8):
                strip_copy(t, kk).start()

    def hand_over(t):
        for dx in (1, 3, 2):
            kk = ring(-dx, 0)[1]
            arrived(gpiece(t, kk), r_g.at[t, dx, 0])
            send(gpiece(t, kk), gpiece(t, kk), s_g.at[t, dx], r_g.at[t, dx, 1], ring(0, 1)[0])

    spread(1)
    for dx, dc in ((1, 0), (3, 0), (1, 1), (3, 1), (2, 0), (2, 1), (0, 1)):
        to, kk = ring(dx, dc)
        send(chans(x_ref, kk), xpiece(xg, k), s_x.at[dx, dc], r_x.at[dx, dc], to)
    own_x = pltpu.make_async_copy(chans(x_ref, k), xpiece(xg, k), r_x.at[0, 0])
    own_x.start()

    @pl.when(y_hi == 0)
    def _():
        gall[:, :, 0:PAD, :] = jnp.zeros((3, 4, PAD, 256), gall.dtype)

    @pl.when(y_hi == 1)
    def _():
        gall[:, :, PAD + 512 :, :] = jnp.zeros((3, 4, PAD, 256), gall.dtype)

    arrived(wpiece(y, quarter), r_w.at[0, 1])
    for dy in (1, 3, 2, 0):
        for dz in DZ:
            if (dy, dz) != (0, 0):
                send(wpiece(y, quarter), wpiece(y, quarter), s_w.at[dy, dz + 1], r_w2(r_w, dy, dz), block(dy, dz)[0])
    hand_over(1)
    for t in (0, 2):
        arrived(gpiece(t, k), r_g.at[t, 0, 0])
        spread(t)
    own_g.wait()

    def tile_ready(t):
        for dx in range(4):
            arrived(gpiece(t, ring(-dx, 1)[1]), r_g.at[t, dx, 1])
        arrived(gall.at[t, :, pl.ds(pl.multiple_of(jnp.where(y_hi == 1, 0, PAD + 512), 16), 16), :], r_h.at[t])

    def shifts(t):
        valid = {0: row >= 3, 1: row >= 0, 2: row < 29}[t]

        def body(h, carry):
            for b in range(3):
                off = PAD + STEP * (1 - b)
                v = gall[t, h, off : off + 512, :]
                gs[t, b, pl.ds(pl.multiple_of(512 * h, 512), 512), :] = jnp.where(valid, v, jnp.zeros_like(v))
            return carry

        lax.fori_loop(0, 4, body, 0)

    def filter_terms(t):
        a = 2 - t

        def body(b, carry):
            part[a, b] = jnp.dot(xt[...], gs[t, b], preferred_element_type=jnp.float32).reshape(4, 4, 16, 256)
            return carry

        lax.fori_loop(0, 3, body, 0)
        for dy in (1, 3, 2):
            to, yy, _ = block(dy, 0)
            send(part.at[a, :, :, yy, :, 0:128], ry.at[a, dy - 1], s_y.at[a, dy], r_y.at[a, dy], to)
        for n, dz in enumerate((-1, 1, 2)):
            to, _, zz = block(0, dz)
            send(part.at[a, :, lax.rem(zz, 4), :, :, 128:256], rz.at[a, n], s_z.at[a, n], r_z.at[a, n], to)

    def first_sums(a):
        for dy in (1, 3, 2):
            arrived(ry.at[a, dy - 1], r_y.at[a, dy])
        suma[a] = part[a, :, :, y, :, 0:128] + ry[a, 0] + ry[a, 1] + ry[a, 2]
        for n, dz in enumerate((-1, 1, 2)):
            to, _, zz = block(0, dz)
            send(suma.at[a, :, lax.rem(zz, 4)], rz2.at[a, n], s_z2.at[a, n], r_z2.at[a, n], to)
        for n in range(3):
            arrived(rz.at[a, n], r_z.at[a, n])
        sumb[a] = part[a, :, quarter, :, :, 128:256] + rz[a, 0] + rz[a, 1] + rz[a, 2]
        for dy in (1, 3, 2):
            to, yy, _ = block(dy, 0)
            send(sumb.at[a, :, yy], ry2.at[a, dy - 1], s_y2.at[a, dy], r_y2.at[a, dy], to)

    def second_sums(a):
        for n in range(3):
            arrived(rz2.at[a, n], r_z2.at[a, n])
        qsum[a, :, :, 0:128] = suma[a, :, quarter] + rz2[a, 0] + rz2[a, 1] + rz2[a, 2]
        for dy in (1, 3, 2):
            arrived(ry2.at[a, dy - 1], r_y2.at[a, dy])
        qsum[a, :, :, 128:256] = sumb[a, :, y] + ry2[a, 0] + ry2[a, 1] + ry2[a, 2]

    passed = []

    def to_owner(a):
        for s in range(4):
            to = (4 * k + quarter, 4 * y + s)
            src = qsum.at[a, :, 8 * (s // 2) : 8 * (s // 2) + 8, 128 * (s % 2) : 128 * (s % 2) + 128]
            cp = pltpu.make_async_remote_copy(src_ref=src, dst_ref=rl.at[a, turn], send_sem=s_l.at[a, s], recv_sem=r_l.at[a, turn], device_id=to, device_id_type=MESH)
            me = same(to)

            @pl.when(jnp.logical_not(me))
            def _():
                cp.start()

            @pl.when(me)
            def _():
                pltpu.make_async_copy(src, rl.at[a, turn], r_l.at[a, turn]).start()

            passed.append((cp, me))

    own_x.wait()
    for dx, dc in ((1, 0), (3, 0), (1, 1), (3, 1), (2, 0), (2, 1), (0, 1)):
        arrived(xpiece(xg, ring(-dx, -dc)[1]), r_x.at[dx, dc])

    for h in range(4):
        xt[:, 512 * h : 512 * h + 512] = xg[h].T
    tile_ready(1)
    shifts(1)
    filter_terms(1)
    for t in (0, 2):
        hand_over(t)
    tile_ready(0)
    shifts(0)
    filter_terms(0)
    first_sums(1)
    tile_ready(2)
    shifts(2)
    filter_terms(2)
    second_sums(1)
    to_owner(1)
    first_sums(2)

    for dy in (1, 3, 2, 0):
        for dz in DZ:
            if (dy, dz) != (0, 0):
                _, yy, zz = block(-dy, -dz)
                arrived(wpiece(yy, lax.rem(zz, 4)), r_w2(r_w, dy, dz))

    def back(h, carry):
        rows = pl.ds(pl.multiple_of(512 * h, 512), 512)
        total = jnp.zeros((512, 256), jnp.float32)
        for t in range(3):
            for b in range(3):
                total = total + lax.dot_general(
                    gs[t, b, rows, :], wg[3 * (2 - t) + b], (((1,), (1,)), ((), ())), preferred_element_type=jnp.float32
                )
        gib[h] = total.astype(gib.dtype)
        return carry

    lax.fori_loop(0, 4, back, 0)
    for dx, dc in ((1, 0), (3, 0), (1, 1), (3, 1), (2, 0), (2, 1), (0, 1)):
        to, kk = ring(dx, dc)
        send(xpiece(gib, kk), chans(gi_ref, k), s_o.at[dx, dc], r_o.at[dx, dc], to)
    own_o = pltpu.make_async_copy(xpiece(gib, k), chans(gi_ref, k), r_o.at[0, 0])
    own_o.start()

    first_sums(0)
    second_sums(2)
    to_owner(2)
    second_sums(0)
    to_owner(0)

    for a in (1, 2, 0):
        for m in range(4):
            arrived(rl.at[a, m], r_l.at[a, m])
        fin[3 * a : 3 * a + 3] = (rl[a, 0] + rl[a, 1] + rl[a, 2] + rl[a, 3]) * scale

    def slot(cc):
        return gw_ref.at[
            :,
            pl.ds(pl.multiple_of(16 * lax.div(cc, 4) + 8 * lax.div(lax.rem(cc, 4), 2), 8), 8),
            pl.ds(pl.multiple_of(128 * lax.rem(cc, 2), 128), 128),
        ]

    for n in range(1, 16):
        send(fin, slot(col), s_a.at[n], r_a.at[n], (row, mod(col + n, 16)))
    own_f = pltpu.make_async_copy(fin, slot(col), l_sem)
    own_f.start()

    for dx, dc in ((1, 0), (3, 0), (1, 1), (3, 1), (2, 0), (2, 1), (0, 1)):
        arrived(chans(gi_ref, ring(-dx, -dc)[1]), r_o.at[dx, dc])
    own_o.wait()
    for n in range(1, 16):
        arrived(slot(mod(col - n, 16)), r_a.at[n])
    own_f.wait()
    for cp in sends:
        cp.wait_send()

    @pl.when(jnp.logical_not(w_self))
    def _():
        w_remote.wait_send()

    for cp, me in passed:

        @pl.when(jnp.logical_not(me))
        def _():
            cp.wait_send()

    @pl.when(is_edge)
    def _():
        for t in range(3):
            for kk in range(8):
                strip_copy(t, kk).wait_send()


def r_w2(r_w, dy, dz):
    return r_w.at[dy, dz + 1]


def shards(inputs, output_gradient, weight):
    height, width, in_chans = inputs.shape
    total = height * width * lax.axis_size("row") * lax.axis_size("col")
    bf, f32 = jnp.bfloat16, jnp.float32
    dma = pltpu.SemaphoreType.DMA
    scratch = [
        pltpu.VMEM((3, 4, 2 * PAD + 512, 256), bf),
        pltpu.VMEM((3, 3, 2048, 256), bf),
        pltpu.VMEM((4, 512, 256), bf),
        pltpu.VMEM((256, 2048), bf),
        pltpu.VMEM((9, 256, 256), bf),
        pltpu.VMEM((3, 3, 4, 4, 16, 256), f32),
        pltpu.VMEM((3, 3, 3, 4, 16, 128), f32),
        pltpu.VMEM((3, 3, 3, 4, 16, 128), f32),
        pltpu.VMEM((3, 3, 4, 16, 128), f32),
        pltpu.VMEM((3, 3, 4, 16, 128), f32),
        pltpu.VMEM((3, 3, 3, 16, 128), f32),
        pltpu.VMEM((3, 3, 3, 16, 128), f32),
        pltpu.VMEM((3, 3, 16, 256), f32),
        pltpu.VMEM((3, 4, 3, 8, 128), f32),
        pltpu.VMEM((9, 8, 128), f32),
        pltpu.VMEM((4, 512, 256), bf),
        dma((3, 4)), dma((3, 4, 2)), dma((3, 4)), dma((3, 8)), dma((3,)),
        dma((4, 2)), dma((4, 2)), dma((4, 4)), dma((4, 4)),
        dma((3, 4)), dma((3, 4)), dma((3, 3)), dma((3, 3)), dma((3, 4)), dma((3, 4)), dma((3, 3)), dma((3, 3)),
        dma((3, 4)), dma((3, 4)), dma((16,)), dma((16,)), dma((4, 2)), dma((4, 2)), dma,
    ]
    hbm = pl.BlockSpec(memory_space=pl.ANY)
    grad_in, grad_weight = pl.pallas_call(
        functools.partial(kernel, 1.0 / math.sqrt(total)),
        out_shape=(jax.ShapeDtypeStruct(inputs.shape, bf), jax.ShapeDtypeStruct((9,) + weight.shape[2:], f32)),
        in_specs=[hbm] * 3,
        out_specs=(hbm, hbm),
        scratch_shapes=scratch,
        compiler_params=pltpu.CompilerParams(collective_id=0, has_side_effects=True, vmem_limit_bytes=56 * 1024 * 1024),
    )(inputs, output_gradient, weight.reshape((9,) + weight.shape[2:]))
    return grad_in, grad_weight.reshape(weight.shape)


def solution(mesh):
    return jax.shard_map(
        shards,
        mesh=mesh,
        in_specs=(P("row", "col", None), P("row", "col", None), P(None, None, "row", None)),
        out_specs=(P("row", "col", None), P(None, None, "row", None)),
        check_vma=False,
    )
```

```python
import functools
import math

import jax
import jax.numpy as jnp
from jax import lax
from jax.experimental import pallas as pl
from jax.experimental.pallas import tpu as pltpu
from jax.sharding import PartitionSpec as P

MESH = pl.DeviceIdType.MESH
STEP = 12
PAD = 16
DZ = (-1, 0, 1, 2)


def mod(a, n):
    return lax.rem(a + 4 * n, n)


def kernel(scale, x_ref, g_ref, w_ref, gi_ref, gw_ref, gall, gs, xg, xt, wg, part, ry, rz, suma, sumb, rz2, ry2, qsum, rl, fin, gib,
           s_g, r_g, s_f, s_h, r_h, s_x, r_x, s_w, r_w, s_y, r_y, s_z, r_z, s_y2, r_y2, s_z2, r_z2, s_l, r_l, s_a, r_a, s_o, r_o, l_sem):
    row, col = lax.axis_index("row"), lax.axis_index("col")
    z, y_lo = lax.rem(row, 16), lax.div(row, 16)
    k, y_hi = lax.rem(col, 8), lax.div(col, 8)
    x, c = lax.div(k, 2), lax.rem(k, 2)
    y = 2 * y_hi + y_lo
    sgn = 1 - 2 * c

    def dev(xx, yy, zz, cc):
        return (lax.rem(yy, 2) * 16 + zz, lax.div(yy, 2) * 8 + 2 * xx + cc)

    def ring(dx, dc):
        xx, cc = mod(x + dx, 4), mod(c + dc, 2)
        return dev(xx, y, z, cc), 2 * xx + cc

    def block(dy, dz):
        yy, zz = mod(y + dy, 4), mod(z + sgn * dz, 16)
        return dev(x, yy, zz, c), yy, zz

    quarter, turn = lax.rem(z, 4), lax.div(z, 4)
    line_k, line_y = lax.div(row, 4), lax.rem(row, 4)
    line_q, line_s = lax.div(col, 4), lax.rem(col, 4)

    def line(m):
        return dev(lax.div(line_k, 2), line_y, 4 * m + line_q, lax.rem(line_k, 2))

    def holder(m):
        kk = lax.div(row, 4)
        return dev(lax.div(kk, 2), lax.div(col, 4), 4 * m + quarter, lax.rem(kk, 2))

    def same(d):
        return jnp.logical_and(d[0] == row, d[1] == col)

    barrier = pltpu.get_barrier_semaphore()

    def greet(d):
        pl.semaphore_signal(barrier, inc=1, device_id=d, device_id_type=MESH)

    greet((4 * k + y, 4 * quarter + turn))
    for m in range(4):
        greet(holder(m))
    greet((mod(row + 3, 32), col))
    greet((mod(row - 3, 32), col))
    for dy in range(4):
        for dz in DZ:
            if (dy, dz) != (0, 0):
                greet(block(-dy, -dz)[0])
    for n in range(1, 16):
        greet((row, mod(col + n, 16)))
    pl.semaphore_wait(barrier, 15 + 15 + 2 + 1 + 4)

    sends = []

    def send(src, dst, ss, rs, d):
        cp = pltpu.make_async_remote_copy(src_ref=src, dst_ref=dst, send_sem=ss, recv_sem=rs, device_id=d, device_id_type=MESH)
        cp.start()
        sends.append(cp)

    def arrived(dst, rs):
        pltpu.make_async_remote_copy(src_ref=dst, dst_ref=dst, send_sem=rs, recv_sem=rs, device_id=ring(0, 1)[0], device_id_type=MESH).wait_recv()

    def gpiece(t, kk):
        return gall.at[t, :, pl.ds(pl.multiple_of(PAD + 64 * kk, 16), 64), :]

    def xpiece(ref, kk):
        return ref.at[:, pl.ds(pl.multiple_of(64 * kk, 64), 64), :]

    def chans(ref, kk):
        return ref.at[:, :, pl.ds(pl.multiple_of(256 * kk, 256), 256)]

    def wpiece(i, p):
        return wg.at[:, pl.ds(pl.multiple_of(64 * i + 16 * p, 16), 16), :]

    send(g_ref, gpiece(0, k), s_g.at[0, 0], r_g.at[0, 0, 0], (mod(row + 3, 32), col))
    send(g_ref, gpiece(2, k), s_g.at[2, 0], r_g.at[2, 0, 0], (mod(row - 3, 32), col))
    own_g = pltpu.make_async_copy(g_ref, gpiece(1, k), r_g.at[1, 0, 0])
    own_g.start()
    w_to = (line(line_s), line_y, line_q)
    w_src = w_ref.at[:, pl.ds(pl.multiple_of(16 * line_q, 16), 16), :]
    w_self = same(w_to[0])
    w_remote = pltpu.make_async_remote_copy(src_ref=w_src, dst_ref=wpiece(line_y, line_q), send_sem=s_w.at[0, 1], recv_sem=r_w.at[0, 1], device_id=w_to[0], device_id_type=MESH)

    @pl.when(jnp.logical_not(w_self))
    def _():
        w_remote.start()

    @pl.when(w_self)
    def _():
        pltpu.make_async_copy(w_src, wpiece(line_y, line_q), r_w.at[0, 1]).start()

    is_edge = jnp.logical_or(jnp.logical_and(y_hi == 1, k == 0), jnp.logical_and(y_hi == 0, k == 7))
    edge_from = jnp.where(y_hi == 1, 0, 48)
    edge_to = jnp.where(y_hi == 1, PAD + 512, 0)
    other = 1 - y_hi

    def strip_copy(t, kk):
        if t == 1:
            src = g_ref.at[:, pl.ds(pl.multiple_of(edge_from, 16), 16), :]
        else:
            src = gall.at[t, :, pl.ds(pl.multiple_of(PAD + 64 * k + edge_from, 16), 16), :]
        dst = gall.at[t, :, pl.ds(pl.multiple_of(edge_to, 16), 16), :]
        return pltpu.make_async_remote_copy(src_ref=src, dst_ref=dst, send_sem=s_h.at[t, kk], recv_sem=r_h.at[t], device_id=(row, 8 * other + kk), device_id_type=MESH)

    def spread(t):
        src = g_ref if t == 1 else gpiece(t, k)
        for dx in (1, 3, 2):
            send(src, gpiece(t, k), s_f.at[t, dx], r_g.at[t, dx, 0], ring(dx, 0)[0])
        send(src, gpiece(t, k), s_f.at[t, 0], r_g.at[t, 0, 1], ring(0, 1)[0])

        @pl.when(is_edge)
        def _():
            for kk in range(8):
                strip_copy(t, kk).start()

    def hand_over(t):
        for dx in (1, 3, 2):
            kk = ring(-dx, 0)[1]
            arrived(gpiece(t, kk), r_g.at[t, dx, 0])
            send(gpiece(t, kk), gpiece(t, kk), s_g.at[t, dx], r_g.at[t, dx, 1], ring(0, 1)[0])

    spread(1)
    for dx, dc in ((1, 0), (3, 0), (1, 1), (3, 1), (2, 0), (2, 1), (0, 1)):
        to, kk = ring(dx, dc)
        send(chans(x_ref, kk), xpiece(xg, k), s_x.at[dx, dc], r_x.at[dx, dc], to)
    own_x = pltpu.make_async_copy(chans(x_ref, k), xpiece(xg, k), r_x.at[0, 0])
    own_x.start()

    @pl.when(y_hi == 0)
    def _():
        gall[:, :, 0:PAD, :] = jnp.zeros((3, 4, PAD, 256), gall.dtype)

    @pl.when(y_hi == 1)
    def _():
        gall[:, :, PAD + 512 :, :] = jnp.zeros((3, 4, PAD, 256), gall.dtype)

    arrived(wpiece(y, quarter), r_w.at[0, 1])
    for dy in (1, 3, 2, 0):
        for dz in DZ:
            if (dy, dz) != (0, 0):
                send(wpiece(y, quarter), wpiece(y, quarter), s_w.at[dy, dz + 1], r_w2(r_w, dy, dz), block(dy, dz)[0])
    hand_over(1)
    for t in (0, 2):
        arrived(gpiece(t, k), r_g.at[t, 0, 0])
        spread(t)
    own_g.wait()

    def tile_ready(t):
        for dx in range(4):
            arrived(gpiece(t, ring(-dx, 1)[1]), r_g.at[t, dx, 1])
        arrived(gall.at[t, :, pl.ds(pl.multiple_of(jnp.where(y_hi == 1, 0, PAD + 512), 16), 16), :], r_h.at[t])

    def shifts(t):
        valid = {0: row >= 3, 1: row >= 0, 2: row < 29}[t]

        def body(h, carry):
            for b in range(3):
                off = PAD + STEP * (1 - b)
                v = gall[t, h, off : off + 512, :]
                gs[t, b, pl.ds(pl.multiple_of(512 * h, 512), 512), :] = jnp.where(valid, v, jnp.zeros_like(v))
            return carry

        lax.fori_loop(0, 4, body, 0)

    def filter_terms(t):
        a = 2 - t

        def body(b, carry):
            part[a, b] = jnp.dot(xt[...], gs[t, b], preferred_element_type=jnp.float32).reshape(4, 4, 16, 256)
            return carry

        lax.fori_loop(0, 3, body, 0)
        for dy in (1, 3, 2):
            to, yy, _ = block(dy, 0)
            send(part.at[a, :, :, yy, :, 0:128], ry.at[a, dy - 1], s_y.at[a, dy], r_y.at[a, dy], to)
        for n, dz in enumerate((-1, 1, 2)):
            to, _, zz = block(0, dz)
            send(part.at[a, :, lax.rem(zz, 4), :, :, 128:256], rz.at[a, n], s_z.at[a, n], r_z.at[a, n], to)

    def first_sums(a):
        for dy in (1, 3, 2):
            arrived(ry.at[a, dy - 1], r_y.at[a, dy])
        suma[a] = part[a, :, :, y, :, 0:128] + ry[a, 0] + ry[a, 1] + ry[a, 2]
        for n, dz in enumerate((-1, 1, 2)):
            to, _, zz = block(0, dz)
            send(suma.at[a, :, lax.rem(zz, 4)], rz2.at[a, n], s_z2.at[a, n], r_z2.at[a, n], to)
        for n in range(3):
            arrived(rz.at[a, n], r_z.at[a, n])
        sumb[a] = part[a, :, quarter, :, :, 128:256] + rz[a, 0] + rz[a, 1] + rz[a, 2]
        for dy in (1, 3, 2):
            to, yy, _ = block(dy, 0)
            send(sumb.at[a, :, yy], ry2.at[a, dy - 1], s_y2.at[a, dy], r_y2.at[a, dy], to)

    def second_sums(a):
        for n in range(3):
            arrived(rz2.at[a, n], r_z2.at[a, n])
        qsum[a, :, :, 0:128] = suma[a, :, quarter] + rz2[a, 0] + rz2[a, 1] + rz2[a, 2]
        for dy in (1, 3, 2):
            arrived(ry2.at[a, dy - 1], r_y2.at[a, dy])
        qsum[a, :, :, 128:256] = sumb[a, :, y] + ry2[a, 0] + ry2[a, 1] + ry2[a, 2]

    passed = []

    def to_owner(a):
        for s in range(4):
            to = (4 * k + quarter, 4 * y + s)
            src = qsum.at[a, :, 8 * (s // 2) : 8 * (s // 2) + 8, 128 * (s % 2) : 128 * (s % 2) + 128]
            cp = pltpu.make_async_remote_copy(src_ref=src, dst_ref=rl.at[a, turn], send_sem=s_l.at[a, s], recv_sem=r_l.at[a, turn], device_id=to, device_id_type=MESH)
            me = same(to)

            @pl.when(jnp.logical_not(me))
            def _():
                cp.start()

            @pl.when(me)
            def _():
                pltpu.make_async_copy(src, rl.at[a, turn], r_l.at[a, turn]).start()

            passed.append((cp, me))

    own_x.wait()
    for dx, dc in ((1, 0), (3, 0), (1, 1), (3, 1), (2, 0), (2, 1), (0, 1)):
        arrived(xpiece(xg, ring(-dx, -dc)[1]), r_x.at[dx, dc])

    for h in range(4):
        xt[:, 512 * h : 512 * h + 512] = xg[h].T
    tile_ready(1)
    shifts(1)
    filter_terms(1)
    for t in (0, 2):
        hand_over(t)
    tile_ready(0)
    shifts(0)
    filter_terms(0)
    first_sums(1)
    tile_ready(2)
    shifts(2)
    filter_terms(2)
    second_sums(1)
    to_owner(1)
    first_sums(2)

    for dy in (1, 3, 2, 0):
        for dz in DZ:
            if (dy, dz) != (0, 0):
                _, yy, zz = block(-dy, -dz)
                arrived(wpiece(yy, lax.rem(zz, 4)), r_w2(r_w, dy, dz))

    def back(h, carry):
        rows = pl.ds(pl.multiple_of(512 * h, 512), 512)
        total = jnp.zeros((512, 256), jnp.float32)
        for t in range(3):
            for b in range(3):
                total = total + lax.dot_general(
                    gs[t, b, rows, :], wg[3 * (2 - t) + b], (((1,), (1,)), ((), ())), preferred_element_type=jnp.float32
                )
        gib[h] = total.astype(gib.dtype)
        return carry

    lax.fori_loop(0, 4, back, 0)
    for dx, dc in ((1, 0), (3, 0), (1, 1), (3, 1), (2, 0), (2, 1), (0, 1)):
        to, kk = ring(dx, dc)
        send(xpiece(gib, kk), chans(gi_ref, k), s_o.at[dx, dc], r_o.at[dx, dc], to)
    own_o = pltpu.make_async_copy(xpiece(gib, k), chans(gi_ref, k), r_o.at[0, 0])
    own_o.start()

    first_sums(0)
    second_sums(2)
    to_owner(2)
    second_sums(0)
    to_owner(0)

    for a in (1, 2, 0):
        for m in range(4):
            arrived(rl.at[a, m], r_l.at[a, m])
        fin[3 * a : 3 * a + 3] = (rl[a, 0] + rl[a, 1] + rl[a, 2] + rl[a, 3]) * scale

    def slot(cc):
        return gw_ref.at[
            :,
            pl.ds(pl.multiple_of(16 * lax.div(cc, 4) + 8 * lax.div(lax.rem(cc, 4), 2), 8), 8),
            pl.ds(pl.multiple_of(128 * lax.rem(cc, 2), 128), 128),
        ]

    for n in range(1, 16):
        send(fin, slot(col), s_a.at[n], r_a.at[n], (row, mod(col + n, 16)))
    own_f = pltpu.make_async_copy(fin, slot(col), l_sem)
    own_f.start()

    for dx, dc in ((1, 0), (3, 0), (1, 1), (3, 1), (2, 0), (2, 1), (0, 1)):
        arrived(chans(gi_ref, ring(-dx, -dc)[1]), r_o.at[dx, dc])
    own_o.wait()
    for n in range(1, 16):
        arrived(slot(mod(col - n, 16)), r_a.at[n])
    own_f.wait()
    for cp in sends:
        cp.wait_send()

    @pl.when(jnp.logical_not(w_self))
    def _():
        w_remote.wait_send()

    for cp, me in passed:

        @pl.when(jnp.logical_not(me))
        def _():
            cp.wait_send()

    @pl.when(is_edge)
    def _():
        for t in range(3):
            for kk in range(8):
                strip_copy(t, kk).wait_send()


def r_w2(r_w, dy, dz):
    return r_w.at[dy, dz + 1]


def shards(inputs, output_gradient, weight):
    height, width, in_chans = inputs.shape
    total = height * width * lax.axis_size("row") * lax.axis_size("col")
    bf, f32 = jnp.bfloat16, jnp.float32
    dma = pltpu.SemaphoreType.DMA
    scratch = [
        pltpu.VMEM((3, 4, 2 * PAD + 512, 256), bf),
        pltpu.VMEM((3, 3, 2048, 256), bf),
        pltpu.VMEM((4, 512, 256), bf),
        pltpu.VMEM((256, 2048), bf),
        pltpu.VMEM((9, 256, 256), bf),
        pltpu.VMEM((3, 3, 4, 4, 16, 256), f32),
        pltpu.VMEM((3, 3, 3, 4, 16, 128), f32),
        pltpu.VMEM((3, 3, 3, 4, 16, 128), f32),
        pltpu.VMEM((3, 3, 4, 16, 128), f32),
        pltpu.VMEM((3, 3, 4, 16, 128), f32),
        pltpu.VMEM((3, 3, 3, 16, 128), f32),
        pltpu.VMEM((3, 3, 3, 16, 128), f32),
        pltpu.VMEM((3, 3, 16, 256), f32),
        pltpu.VMEM((3, 4, 3, 8, 128), f32),
        pltpu.VMEM((9, 8, 128), f32),
        pltpu.VMEM((4, 512, 256), bf),
        dma((3, 4)), dma((3, 4, 2)), dma((3, 4)), dma((3, 8)), dma((3,)),
        dma((4, 2)), dma((4, 2)), dma((4, 4)), dma((4, 4)),
        dma((3, 4)), dma((3, 4)), dma((3, 3)), dma((3, 3)), dma((3, 4)), dma((3, 4)), dma((3, 3)), dma((3, 3)),
        dma((3, 4)), dma((3, 4)), dma((16,)), dma((16,)), dma((4, 2)), dma((4, 2)), dma,
    ]
    hbm = pl.BlockSpec(memory_space=pl.ANY)
    grad_in, grad_weight = pl.pallas_call(
        functools.partial(kernel, 1.0 / math.sqrt(total)),
        out_shape=(jax.ShapeDtypeStruct(inputs.shape, bf), jax.ShapeDtypeStruct((9,) + weight.shape[2:], f32)),
        in_specs=[hbm] * 3,
        out_specs=(hbm, hbm),
        scratch_shapes=scratch,
        compiler_params=pltpu.CompilerParams(collective_id=0, has_side_effects=True, vmem_limit_bytes=56 * 1024 * 1024),
    )(inputs, output_gradient, weight.reshape((9,) + weight.shape[2:]))
    return grad_in, grad_weight.reshape(weight.shape)


def solution(mesh):
    return jax.shard_map(
        shards,
        mesh=mesh,
        in_specs=(P("row", "col", None), P("row", "col", None), P(None, None, "row", None)),
        out_specs=(P("row", "col", None), P(None, None, "row", None)),
        check_vma=False,
    )
```
